256 devices in a mesh: req: 16 (over z, core), mp: 16 (over x, y).
Axes of the slice: x: 4, y: 4, z: 8, core: 2. Of those that a mesh axis runs over, the one named last changes fastest.
Arguments:
- tokens: bfloat16 [1568, 7168], P('req', 'mp'), may hold values from -6 to 6
- layernorm_scale: float32 [7168], replicated, may hold values from 0.5 to 1.5
- layernorm_bias: float32 [7168], replicated, may hold values from -3 to 3
- query_key_value_weight: bfloat16 [3, 7168, 6144], P(None, 'req', 'mp'), may hold values from -0.0625 to 0.0625
- query_key_value_bias: float32 [3, 6144], P(None, 'mp'), may hold values from -3 to 3
- adapter_down_weight: bfloat16 [64, 7168, 32], P('req', 'mp'), may hold values from -0.0625 to 0.0625
- adapter_up_weight: bfloat16 [64, 2, 16, 6144], P('req', None, None, 'mp'), may hold values from -1.5 to 1.5
- adapter_index_table: int32 [16, 5], P('req'), may hold values from 0 to 63
- prompt_length_list: int32 [48], P('req'), may hold values from 1 to 32, 960 in all
- cache: bfloat16 [32, 2048, 2, 6144], P('req', None, None, 'mp'), may hold values from -320 to 320, as said below
- cache_length_list: int32 [32], P('req'), may hold values from 1 to 2048, 20480 in all
- output_weight: bfloat16 [6144, 7168], P('mp', 'req'), may hold values from -0.078125 to 0.078125
- output_bias: float32 [7168], P('mp'), may hold values from -3 to 3
Outputs:
- layer_out: bfloat16 [1568, 7168], P('req', 'mp')
The draws below stay inside these ranges and needn't reach their ends.
Inputs may be any that keep to these rules, and one draw needn't show every extreme that they name: Each prompt fills the first prompt_length_list rows of its slot of 32 rows. Live cache positions are the first cache_length_list of each slot. `cache`: entries mostly of order one, though rare keys may be larger.
All inputs are finite; a program needn't handle non-finite values. No bound on the sum of `prompt_length_list` or of `cache_length_list` on one device may be relied on, other than what follows from the above.
Results may differ from the reference program's by a relative error of at most 0.015.
Values may be sent and summed in bfloat16 or wider, within the bound.
A program may use at most 128 MiB of HBM per device.

```python
import math
import jax
import jax.numpy as jnp
import numpy as np
from jax import lax

MODEL_WIDTH = 7168
HEAD_DIM = 128
HEADS = 48
ADAPTER_RANK = 16
ADAPTER_COUNT = 64
DEC_DEV = 2
PSLOTS = 3
PLEN = 32
CACHE = 2048
HEAD_FEATURES = 6144
ROWS = 1568
PROMPTS = 48
DECODES = 32
N_REQ = 16


def draw_cache(key, part):
    main_key = jax.random.fold_in(key, 0)
    entries = jnp.clip(jax.random.normal(main_key, (DECODES, CACHE, 2, HEADS * HEAD_DIM), jnp.float32), -8.0, 8.0)
    return entries.astype(jnp.bfloat16)


def plant(drawn, stream_key, low, largest):
    index_at = [jax.random.randint(jax.random.fold_in(stream_key, axis), (), 0, length) for axis, length in enumerate(drawn.shape)]
    main_axis = drawn.shape.index(max(drawn.shape))
    next_to = index_at[:main_axis] + [(index_at[main_axis] + 1) % drawn.shape[main_axis]] + index_at[main_axis + 1:]
    return drawn.at[tuple(index_at)].set(low).at[tuple(next_to)].set(largest)


def steps_of(stream_key, extent, cuts, low, high):
    loudness, own = 1.0, jax.random.fold_in(stream_key, 6)
    for position, parts in cuts:
        draws = jnp.exp(jax.random.uniform(jax.random.fold_in(own, position), (parts,), jnp.float32, low / len(cuts), high / len(cuts)))
        loudness = loudness * jnp.repeat(draws, extent[position] // parts).reshape([-1 if axis == position else 1 for axis in range(len(extent))])
    return loudness


def rank_bounds(number_of, lean):
    loads = [(1 << 20) // math.isqrt(grade ** lean) + 1 for grade in range(1, number_of + 1)]
    width = 1 + sum(loads) // (1 << 30)
    return np.cumsum(np.array([max(1, weight // width) for weight in loads]))


def ranked(rng, shape, count, slope):
    table = rank_bounds(count, slope)
    ticket = jax.random.randint(jax.random.fold_in(rng, 1), shape, 0, int(table[count - 1]))
    grade = jnp.searchsorted(jnp.asarray(table, jnp.int32), ticket, side="right")
    return jax.random.permutation(jax.random.fold_in(rng, 2), count)[grade].astype(jnp.int32)


def split_up(amount, total, bound, skew):
    weights = [(1 << 20) // math.isqrt(standing ** skew) + 1 for standing in range(2, amount + 1)]
    spare, holding = total - bound - (amount - 1), [1] * (amount - 1)
    while spare > 0:
        free = [i for i in range(amount - 1) if holding[i] < bound]
        pool, remaining = sum([weights[i] for i in free]), spare
        for i in free:
            addition = min(bound - holding[i], max(1, remaining * weights[i] // pool), spare)
            holding[i] = holding[i] + addition
            spare = spare - addition
    return np.array([bound] + holding)


def ragged_sizes(key, count, total, limit, lean):
    if count == 2:
        one = jax.random.randint(key, (), max(1, total - limit), min(limit, total - 1) + 1)
        return jnp.stack([one, total - one])
    tallies = jnp.asarray(split_up(count, total, limit, lean), jnp.int32)
    couples = (count - 1) // 2
    giver, taker = tallies[1:1 + 2 * couples:2], tallies[2:2 + 2 * couples:2]
    room = jnp.minimum(giver - 1, limit - taker)
    moved = jax.random.randint(jax.random.fold_in(key, 1), (couples,), 0, 1 << 20) % (room + 1)
    tallies = tallies.at[1:1 + 2 * couples:2].set(giver - moved).at[2:2 + 2 * couples:2].set(taker + moved)
    return tallies[jax.random.permutation(jax.random.fold_in(key, 2), count)]


def gaussian(stream_key, dims, spread, most, cuts=(), dtype=jnp.bfloat16):
    level = steps_of(stream_key, dims, cuts, -0.22, 0.18) if cuts else 1.0
    drawn = jax.random.normal(stream_key, dims, jnp.float32) * spread * level
    return jnp.minimum(jnp.maximum(drawn, -most), most).astype(dtype)


def setup_inputs(seed: int = 0) -> dict:
    key_of = jax.random.split(jax.random.key(seed), 14)
    tokens = gaussian(key_of[0], (ROWS, MODEL_WIDTH), 1.0, 6.0, ((0, 16), (1, 16)))
    layernorm_scale = jnp.clip(1.0 + 0.1 * jax.random.normal(key_of[1], (MODEL_WIDTH,), jnp.float32), 0.5, 1.5)
    layernorm_bias = gaussian(key_of[2], (MODEL_WIDTH,), 0.5, 3.0, (), jnp.float32)
    query_key_value_weight = gaussian(key_of[3], (3, MODEL_WIDTH, HEAD_FEATURES), MODEL_WIDTH ** -0.5, 0.0625, ((1, 16), (2, 16)))
    query_key_value_bias = gaussian(key_of[4], (3, HEAD_FEATURES), 0.5, 3.0, ((1, 16),), jnp.float32)
    adapter_down_weight = gaussian(key_of[5], (ADAPTER_COUNT, MODEL_WIDTH, 2 * ADAPTER_RANK), MODEL_WIDTH ** -0.5, 0.0625, ((0, 16), (1, 16)))
    adapter_up_weight = gaussian(key_of[6], (ADAPTER_COUNT, 2, ADAPTER_RANK, HEAD_FEATURES), ADAPTER_RANK ** -0.5, 1.5, ((0, 16), (3, 16)))
    adapter_index_table = plant(ranked(key_of[7], (N_REQ, PSLOTS + DEC_DEV), ADAPTER_COUNT, 2), jax.random.fold_in(key_of[7], 3), 0, ADAPTER_COUNT - 1).astype(jnp.int32)
    prompt_length_list = ragged_sizes(key_of[8], PROMPTS, PROMPTS * PLEN * 5 // 8, PLEN, 1).astype(jnp.int32)
    cache = draw_cache(jax.random.fold_in(key_of[13], 71), 0)
    cache_length_list = ragged_sizes(key_of[10], DECODES, DECODES * CACHE * 5 // 16, CACHE, 1).astype(jnp.int32)
    output_weight = gaussian(key_of[11], (HEAD_FEATURES, MODEL_WIDTH), HEAD_FEATURES ** -0.5, 0.078125, ((0, 16), (1, 16)))
    output_bias = gaussian(key_of[12], (MODEL_WIDTH,), 0.5, 3.0, ((0, 16),), jnp.float32)
    return dict(tokens=tokens, layernorm_scale=layernorm_scale, layernorm_bias=layernorm_bias, query_key_value_weight=query_key_value_weight, query_key_value_bias=query_key_value_bias, adapter_down_weight=adapter_down_weight, adapter_up_weight=adapter_up_weight, adapter_index_table=adapter_index_table, prompt_length_list=prompt_length_list, cache=cache, cache_length_list=cache_length_list, output_weight=output_weight, output_bias=output_bias)


def layer_norm(row_data, gain_vec, shift_vec):
    values = row_data.astype(jnp.float32)
    average = lax.optimization_barrier(jnp.mean(values, axis=-1, keepdims=True))
    centred = values - average
    variance = lax.optimization_barrier(jnp.mean(centred * centred, axis=-1, keepdims=True))
    scaled = centred * lax.rsqrt(variance + 1e-05)
    return (scaled * gain_vec + shift_vec).astype(jnp.bfloat16)

def reference(tokens, layernorm_scale, layernorm_bias, query_key_value_weight, query_key_value_bias, adapter_down_weight, adapter_up_weight, adapter_index_table, prompt_length_list, cache, cache_length_list, output_weight, output_bias):
    prompt_rows = PSLOTS * PLEN
    rows_dev = prompt_rows + DEC_DEV
    combined_width = HEADS * HEAD_DIM
    score_scale = HEAD_DIM ** (-0.5)
    normed = layer_norm(tokens, layernorm_scale, layernorm_bias)
    projected = jnp.stack([jnp.dot(normed, query_key_value_weight[adapter_membership], preferred_element_type=jnp.float32) for adapter_membership in range(3)], axis=1)
    projected = projected + query_key_value_bias[None]
    positions = jnp.arange(rows_dev)
    request_slot = jnp.where(positions < prompt_rows, positions // PLEN, PSLOTS + positions - prompt_rows).astype(jnp.int32)
    row_adapter = adapter_index_table[:, request_slot].reshape(-1)
    selection_mask = (row_adapter[:, None] == jnp.arange(ADAPTER_COUNT)[None, :]).astype(jnp.float32)
    down_weight_flat = jnp.transpose(adapter_down_weight, (1, 0, 2)).reshape(MODEL_WIDTH, ADAPTER_COUNT * 2 * ADAPTER_RANK)
    adapter_wise_sums = jnp.dot(normed, down_weight_flat, preferred_element_type=jnp.float32).reshape(-1, ADAPTER_COUNT, 2 * ADAPTER_RANK)
    reduced_rank_rows = jnp.einsum('na,nae->ne', selection_mask, adapter_wise_sums).astype(jnp.bfloat16)
    broadcast_rank_rows = (selection_mask.astype(jnp.bfloat16)[:, :, None] * reduced_rank_rows[:, None, :]).reshape(-1, ADAPTER_COUNT, 2, ADAPTER_RANK)
    deltas = []
    for adapter_membership in range(2):
        part_rank = broadcast_rank_rows[:, :, adapter_membership].reshape(-1, ADAPTER_COUNT * ADAPTER_RANK)
        up_weight_flat = adapter_up_weight[:, adapter_membership].reshape(ADAPTER_COUNT * ADAPTER_RANK, combined_width)
        rounded = jnp.dot(part_rank, up_weight_flat, preferred_element_type=jnp.float32).astype(jnp.bfloat16)
        deltas.append(lax.optimization_barrier(rounded).astype(jnp.float32))
    queries = (projected[:, 0] + deltas[0]).astype(jnp.bfloat16)
    keys_new = projected[:, 1].astype(jnp.bfloat16)
    values_new = (projected[:, 2] + deltas[1]).astype(jnp.bfloat16)
    grid_q = queries.reshape(N_REQ, rows_dev, HEADS, HEAD_DIM)
    grid_k = keys_new.reshape(N_REQ, rows_dev, HEADS, HEAD_DIM)
    grid_v = values_new.reshape(N_REQ, rows_dev, HEADS, HEAD_DIM)
    prompt_q = grid_q[:, :prompt_rows].reshape(N_REQ * PSLOTS, PLEN, HEADS, HEAD_DIM)
    prompt_k = grid_k[:, :prompt_rows].reshape(N_REQ * PSLOTS, PLEN, HEADS, HEAD_DIM)
    prompt_v = grid_v[:, :prompt_rows].reshape(N_REQ * PSLOTS, PLEN, HEADS, HEAD_DIM)
    causal = jnp.arange(PLEN)[None, :] <= jnp.arange(PLEN)[:, None]

    def one_prompt(item):
        query_blk, key_blk, value_blk, length = item
        scores = jnp.einsum('ihd,jhd->hij', query_blk.astype(jnp.float32), key_blk.astype(jnp.float32)) * score_scale
        scores = jnp.where(causal[None], scores, -1e+30)
        highest = lax.optimization_barrier(jnp.max(scores, axis=2, keepdims=True))
        weights = jnp.where(causal[None], jnp.exp(scores - highest), 0.0)
        weights = (weights / lax.optimization_barrier(jnp.sum(weights, axis=2, keepdims=True))).astype(jnp.bfloat16)
        result = jnp.einsum('hij,jhd->ihd', weights.astype(jnp.float32), value_blk.astype(jnp.float32))
        active = jnp.arange(PLEN) < length
        return jnp.where(active[:, None, None], result, 0.0).astype(jnp.bfloat16)
    prompt_out = lax.map(one_prompt, (prompt_q, prompt_k, prompt_v, prompt_length_list))
    prompt_out = prompt_out.reshape(N_REQ, prompt_rows, combined_width)
    decode_q = grid_q[:, prompt_rows:].reshape(N_REQ * DEC_DEV, HEADS, HEAD_DIM)
    decode_k = grid_k[:, prompt_rows:].reshape(N_REQ * DEC_DEV, HEADS, HEAD_DIM)
    decode_v = grid_v[:, prompt_rows:].reshape(N_REQ * DEC_DEV, HEADS, HEAD_DIM)

    def one_decode(item):
        query_row, key_row, value_row, stored, length = item
        keys_old = stored[:, 0].reshape(CACHE, HEADS, HEAD_DIM).astype(jnp.float32)
        values_old = stored[:, 1].reshape(CACHE, HEADS, HEAD_DIM).astype(jnp.float32)
        query_row = query_row.astype(jnp.float32)
        row_scores = jnp.einsum('hd,thd->ht', query_row, keys_old) * score_scale
        live_cache = jnp.arange(CACHE)[None, :] < length
        row_scores = jnp.where(live_cache, row_scores, -1e+30)
        self_score = lax.optimization_barrier(jnp.sum(query_row * key_row.astype(jnp.float32), axis=1)) * score_scale
        row_top = jnp.maximum(lax.optimization_barrier(jnp.max(row_scores, axis=1)), self_score)
        row_weights = jnp.where(live_cache, jnp.exp(row_scores - row_top[:, None]), 0.0)
        self_weight = jnp.exp(self_score - row_top)
        totals = lax.optimization_barrier(jnp.sum(row_weights, axis=1)) + self_weight
        row_weights = (row_weights / totals[:, None]).astype(jnp.bfloat16)
        self_weight = (self_weight / totals).astype(jnp.bfloat16)
        result = jnp.einsum('ht,thd->hd', row_weights.astype(jnp.float32), values_old)
        result = result + self_weight.astype(jnp.float32)[:, None] * value_row.astype(jnp.float32)
        return result.astype(jnp.bfloat16)
    decode_out = lax.map(one_decode, (decode_q, decode_k, decode_v, cache, cache_length_list))
    decode_out = decode_out.reshape(N_REQ, DEC_DEV, combined_width)
    attended = jnp.concatenate([prompt_out, decode_out], axis=1).reshape(N_REQ * rows_dev, combined_width)
    mixed = jnp.dot(attended, output_weight, preferred_element_type=jnp.float32)
    return (tokens.astype(jnp.float32) + mixed + output_bias[None]).astype(jnp.bfloat16)
```

```python
import functools

import jax
import jax.numpy as jnp
from jax import lax
from jax.experimental import pallas as pl
from jax.experimental.pallas import tpu as pltpu
from jax.sharding import PartitionSpec as P

HEAD_DIM = 128
RANK = 16
NZ = 8
NM = 16
PAD = 112
MESH = pl.DeviceIdType.MESH
F32, BF16 = jnp.float32, jnp.bfloat16
VMEM_SPEC = pl.BlockSpec(memory_space=pltpu.VMEM)
SMEM_SPEC = pl.BlockSpec(memory_space=pltpu.SMEM)
ANY_SPEC = pl.BlockSpec(memory_space=pl.ANY)
LIMIT = 56 * 1024 * 1024


def place():
    r, m = lax.axis_index("req"), lax.axis_index("mp")
    return r // 2, r % 2, m


def at(z, c, m):
    return (z * 2 + c, m)


def signal(sem, device):
    pl.semaphore_signal(sem, inc=1, device_id=device, device_id_type=MESH)


def remote(src, dst, send, recv, device):
    return pltpu.make_async_remote_copy(
        src_ref=src, dst_ref=dst, send_sem=send, recv_sem=recv, device_id=device, device_id_type=MESH
    )


def plane_signal(barrier, z, c, m):
    def body(k, carry):
        signal(barrier, at(z, c, (m + k) % NM))
        return carry

    lax.fori_loop(1, NM, body, 0)


def ring_gather(z, c, m, out, send, recv):
    def step(way, s):
        sign = 1 - 2 * way
        block = (z + NZ - sign * s) % NZ
        target = at((z + NZ + sign) % NZ, c, m)
        return remote(out.at[block], out.at[block], send.at[way, s], recv.at[way, s], target)

    return step


def ring_steps():
    order = []
    for s in range(4):
        order.append((0, s))
        if s < 3:
            order.append((1, s))
    return order


def spread_kernel(
    tok, gains, w, wo, down, up,
    gathered, normed, w_both, wo_both, down_all, up_all,
    stats, tmp, mine, loc_sem, chip_send, chip_recv,
    st_send, st_recv, pm_send, pm_recv, ga_send, ga_recv,
    dn_send, dn_recv, up_send, up_recv, xd_send, xd_recv, xu_send, xu_recv,
):
    z, c, m = place()
    rows, cols = tok.shape
    other = at(z, 1 - c, m)
    tz, tm = m // 2, 2 * z + m % 2
    target = at(tz, c, tm)
    away = tz != z

    barrier = pltpu.get_barrier_semaphore()
    plane_signal(barrier, z, c, m)
    signal(barrier, other)
    signal(barrier, at((z + 1) % NZ, c, m))
    signal(barrier, at((z + NZ - 1) % NZ, c, m))

    @pl.when(away)
    def _():
        signal(barrier, target)

    x = tok[...].astype(F32)
    mean = jnp.sum(x, axis=1, keepdims=True) * (1.0 / cols)
    dev = x - mean
    m2 = jnp.sum(dev * dev, axis=1, keepdims=True)
    lane = lax.broadcasted_iota(jnp.int32, (rows, 128), 1)
    tmp[...] = jnp.zeros_like(tmp)
    tmp[0:rows, :] = jnp.where(lane == 0, mean, jnp.where(lane == 1, m2, 0.0))
    stats[m] = tmp[...].T[0:8, :]

    locals_ = [
        pltpu.make_async_copy(w, w_both.at[c], loc_sem.at[0]),
        pltpu.make_async_copy(wo, wo_both.at[c], loc_sem.at[1]),
        pltpu.make_async_copy(down, down_all.at[c, z], loc_sem.at[2]),
        pltpu.make_async_copy(up, up_all.at[c, z], loc_sem.at[3]),
    ]
    for one in locals_:
        one.start()

    pl.semaphore_wait(barrier, NM + 2 + jnp.minimum(jnp.abs(tz - z), 1))

    def stat(k):
        return remote(stats.at[m], stats.at[m], st_send.at[k], st_recv.at[k], at(z, c, (m + k) % NM))

    def start_stat(k, carry):
        stat(k).start()
        return carry

    lax.fori_loop(1, NM, start_stat, 0)

    locals_[2].wait()
    locals_[3].wait()
    dn_step = ring_gather(z, c, m, down_all.at[c], dn_send, dn_recv)
    up_step = ring_gather(z, c, m, up_all.at[c], up_send, up_recv)

    def cross(block, i):
        return (
            remote(down_all.at[c, block], down_all.at[c, block], xd_send.at[i], xd_recv.at[i], other),
            remote(up_all.at[c, block], up_all.at[c, block], xu_send.at[i], xu_recv.at[i], other),
        )

    for way in range(2):
        dn_step(way, 0).start()
        up_step(way, 0).start()
    for one in cross(z, 0):
        one.start()
    chip = [
        remote(w, w_both.at[c], chip_send.at[0], chip_recv.at[0], other),
        remote(wo, wo_both.at[c], chip_send.at[1], chip_recv.at[1], other),
    ]
    for one in chip:
        one.start()

    def wait_stat(k, carry):
        stat(k).wait()
        return carry

    lax.fori_loop(1, NM, wait_stat, 0)
    every = stats[...]
    means, m2s = every[:, 0, :], every[:, 1, :]
    mean = jnp.sum(means, axis=0, keepdims=True) * (1.0 / NM)
    off = means - mean
    total = jnp.sum(m2s, axis=0, keepdims=True) + cols * jnp.sum(off * off, axis=0, keepdims=True)
    inv = lax.rsqrt(total * (1.0 / (NM * cols)) + 1e-05)
    sub = lax.broadcasted_iota(jnp.int32, (128, 128), 0)
    tmp[...] = jnp.where(sub == 0, mean, jnp.where(sub == 1, inv, 0.0)).T
    both = tmp[0:rows, :]
    g = gains[...]
    value = (x - both[:, 0:1]) * both[:, 1:2] * g[0:1, :] + g[1:2, :]
    normed[...] = jnp.zeros_like(normed)
    normed[0:rows, :] = value.astype(BF16)

    perm = remote(normed, mine, pm_send, pm_recv, target)
    keep = pltpu.make_async_copy(normed, mine, loc_sem.at[4])

    @pl.when(away)
    def _():
        perm.start()
        perm.wait()

    @pl.when(jnp.logical_not(away))
    def _():
        keep.start()
        keep.wait()

    own = pltpu.make_async_copy(mine, gathered.at[m], loc_sem.at[5])
    own.start()

    def share(k):
        return remote(mine, gathered.at[m], ga_send.at[k], ga_recv.at[k], at(z, c, (m + k) % NM))

    def start_share(k, carry):
        share(k).start()
        return carry

    lax.fori_loop(1, NM, start_share, 0)

    i = 1
    for way, s in ring_steps():
        dn_step(way, s).wait()
        up_step(way, s).wait()
        sign = 1 - 2 * way
        if s + 1 < (4, 3)[way]:
            dn_step(way, s + 1).start()
            up_step(way, s + 1).start()
        for one in cross((z + NZ - sign * (s + 1)) % NZ, i):
            one.start()
        i += 1

    def wait_share(k, carry):
        share(k).wait()
        return carry

    lax.fori_loop(1, NM, wait_share, 0)
    own.wait()
    locals_[0].wait()
    locals_[1].wait()
    for one in chip:
        one.wait()
    for one in cross(z, 0):
        one.wait()
    i = 1
    for way, s in ring_steps():
        sign = 1 - 2 * way
        for one in cross((z + NZ - sign * (s + 1)) % NZ, i):
            one.wait()
        i += 1


def spread(tok, gains, w, wo, down, up):
    rows, cols = tok.shape
    dma = pltpu.SemaphoreType.DMA
    shape = jax.ShapeDtypeStruct
    return pl.pallas_call(
        spread_kernel,
        out_shape=(
            shape((NM, PAD, cols), BF16),
            shape((PAD, cols), BF16),
            shape((2, *w.shape), BF16),
            shape((2, *wo.shape), BF16),
            shape((2, NZ, *down.shape), BF16),
            shape((2, NZ, *up.shape), BF16),
        ),
        in_specs=[VMEM_SPEC, VMEM_SPEC, ANY_SPEC, ANY_SPEC, ANY_SPEC, ANY_SPEC],
        out_specs=(VMEM_SPEC, VMEM_SPEC, ANY_SPEC, ANY_SPEC, ANY_SPEC, ANY_SPEC),
        scratch_shapes=[
            pltpu.VMEM((NM, 8, 128), F32),
            pltpu.VMEM((128, 128), F32),
            pltpu.VMEM((PAD, cols), BF16),
            dma((6,)), dma((2,)), dma((2,)),
            dma((NM,)), dma((NM,)), dma, dma, dma((NM,)), dma((NM,)),
            dma((2, 4)), dma((2, 4)), dma((2, 4)), dma((2, 4)),
            dma((8,)), dma((8,)), dma((8,)), dma((8,)),
        ],
        compiler_params=pltpu.CompilerParams(collective_id=0, has_side_effects=True, vmem_limit_bytes=LIMIT),
        name="spread",
    )(tok, gains, w, wo, down, up)


def project_kernel(table, gathered, normed, w_both, down_all, part, low):
    cols = normed.shape[1]
    rows = PAD
    halves = [
        gathered[...].reshape(NZ, 2, rows, cols)[:, f].reshape(NZ * rows, cols) for f in range(2)
    ]
    for comp in range(3):
        acc = jnp.dot(halves[0], w_both[0, comp], preferred_element_type=F32)
        acc = acc + jnp.dot(halves[1], w_both[1, comp], preferred_element_type=F32)
        for h in range(3):
            part[:, comp * 3 + h] = acc[:, h * 128:(h + 1) * 128].reshape(NZ, rows, 128)
    slots = table.shape[1]
    per = down_all.shape[2]
    picked = []
    for s in range(slots):
        a = table[0, s]
        owner = a // per
        picked.append(down_all[owner % 2, owner // 2, a % per])
    stacked = jnp.concatenate(picked, axis=0)
    every = lax.dot_general(
        stacked, normed[...], (((1,), (1,)), ((), ())), preferred_element_type=F32
    )
    lane = lax.broadcasted_iota(jnp.int32, (2 * RANK, rows), 1)
    acc = jnp.zeros((2 * RANK, rows), F32)
    for s in range(slots):
        lo, hi = slot_rows(s)
        acc = jnp.where((lane >= lo) & (lane < hi), every[2 * RANK * s:2 * RANK * (s + 1)], acc)
    low[...] = jnp.zeros_like(low)
    low[:, 0:rows] = acc


def slot_rows(s):
    return (32 * s, 32 * s + 32) if s < 3 else (93 + s, 94 + s)


def project(table, gathered, normed, w_both, down_all):
    shape = jax.ShapeDtypeStruct
    return pl.pallas_call(
        project_kernel,
        out_shape=(shape((NZ, 9, PAD, 128), F32), shape((2 * RANK, 128), F32)),
        in_specs=[SMEM_SPEC, VMEM_SPEC, VMEM_SPEC, VMEM_SPEC, VMEM_SPEC],
        out_specs=(VMEM_SPEC, VMEM_SPEC),
        compiler_params=pltpu.CompilerParams(vmem_limit_bytes=LIMIT),
        name="project",
    )(table, gathered, normed, w_both, down_all)


def reduce_kernel(part, low, sums, lows, out_buf, in_buf, send, recv, lo_send, lo_recv, loc):
    z, c, m = place()
    barrier = pltpu.get_barrier_semaphore()
    plane_signal(barrier, z, c, m)
    signal(barrier, at((z + 1) % NZ, c, m))
    signal(barrier, at((z + NZ - 1) % NZ, c, m))
    pl.semaphore_wait(barrier, NM + 1)

    def ways():
        return [1] * 4 + [1 - 2 * c] + [-1] * 4

    def hop(j, way, s):
        return remote(
            out_buf.at[s, j], in_buf.at[s, j], send.at[s, j], recv.at[s, j], at((z + NZ + way) % NZ, c, m)
        )

    for j, way in enumerate(ways()):
        out_buf[0, j] = part[(z + NZ - way) % NZ, j].astype(BF16)
        hop(j, way, 0).start()

    def give(k):
        return remote(low, lows.at[m], lo_send.at[k], lo_recv.at[k], at(z, c, (m + k) % NM))

    def start_give(k, carry):
        give(k).start()
        return carry

    lax.fori_loop(1, NM, start_give, 0)
    own = pltpu.make_async_copy(low, lows.at[m], loc)
    own.start()

    def step(s, carry):
        for j, way in enumerate(ways()):
            hop(j, way, s - 1).wait_recv()
            block = (z + 2 * NZ - way * (1 + s)) % NZ
            out_buf[s, j] = (in_buf[s - 1, j].astype(F32) + part[block, j]).astype(BF16)
            hop(j, way, s).start()
        return carry

    lax.fori_loop(1, NZ - 1, step, 0)
    for j, way in enumerate(ways()):
        hop(j, way, NZ - 2).wait_recv()
        sums[j] = in_buf[NZ - 2, j].astype(F32) + part[z, j]

    def finish(s, carry):
        for j, way in enumerate(ways()):
            hop(j, way, s).wait_send()
        return carry

    lax.fori_loop(0, NZ - 1, finish, 0)

    def wait_give(k, carry):
        give(k).wait()
        return carry

    lax.fori_loop(1, NM, wait_give, 0)
    own.wait()


def reduce(part, low):
    dma = pltpu.SemaphoreType.DMA
    shape = jax.ShapeDtypeStruct
    return pl.pallas_call(
        reduce_kernel,
        out_shape=(shape((9, PAD, 128), F32), shape((NM, 2 * RANK, 128), F32)),
        in_specs=[VMEM_SPEC, VMEM_SPEC],
        out_specs=(VMEM_SPEC, VMEM_SPEC),
        scratch_shapes=[
            pltpu.VMEM((NZ - 1, 9, PAD, 128), BF16),
            pltpu.VMEM((NZ - 1, 9, PAD, 128), BF16),
            dma((NZ - 1, 9)), dma((NZ - 1, 9)), dma((NM,)), dma((NM,)), dma,
        ],
        compiler_params=pltpu.CompilerParams(collective_id=1, has_side_effects=True, vmem_limit_bytes=LIMIT),
        name="reduce",
    )(part, low)


def attend_kernel(table, lengths, cache_lengths, sums, lows, up_all, bias, cache, out, q_bd):
    rows = PAD
    scale = HEAD_DIM ** (-0.5)
    low = jnp.sum(lows[...], axis=0)[:, 0:rows].astype(BF16)
    slots = table.shape[1]
    per = up_all.shape[2]
    lane = lax.broadcasted_iota(jnp.int32, (RANK, rows), 1)
    deltas = []
    for which in range(2):
        left, right = [], []
        half = low[RANK * which:RANK * (which + 1)]
        for s in range(slots):
            lo, hi = slot_rows(s)
            left.append(jnp.where((lane >= lo) & (lane < hi), half, jnp.zeros((), BF16)))
            a = table[0, s]
            owner = a // per
            right.append(up_all[owner % 2, owner // 2, a % per, which])
        deltas.append(
            lax.dot_general(
                jnp.concatenate(left, axis=0), jnp.concatenate(right, axis=0),
                (((0,), (0,)), ((), ())), preferred_element_type=F32,
            ).astype(BF16).astype(F32)
        )
    ri = lax.broadcasted_iota(jnp.int32, (rows, rows), 0)
    ci = lax.broadcasted_iota(jnp.int32, (rows, rows), 1)
    seen = (ri // 32 == ci // 32) & (ci <= ri)
    row = lax.broadcasted_iota(jnp.int32, (rows, 1), 0)
    live = jnp.zeros((rows, 1), jnp.bool_)
    for s in range(3):
        live = live | ((row >= 32 * s) & (row < 32 * s + lengths[s]))
    qs, ks, vs = [], [], []
    for h in range(3):
        cut = slice(h * 128, (h + 1) * 128)
        qs.append((sums[h] + bias[h] + deltas[0][:, cut]).astype(BF16))
        ks.append((sums[3 + h] + bias[3 + h]).astype(BF16))
        vs.append((sums[6 + h] + bias[6 + h] + deltas[1][:, cut]).astype(BF16))
    span = cache.shape[1]
    q_bd[...] = jnp.zeros_like(q_bd)
    prompt = []
    for h in range(3):
        s = lax.dot_general(qs[h], ks[h], (((1,), (1,)), ((), ())), preferred_element_type=F32) * scale
        s = jnp.where(seen, s, -1e30)
        e = jnp.where(seen, jnp.exp(s - jnp.max(s, axis=1, keepdims=True)), 0.0)
        p = (e / jnp.sum(e, axis=1, keepdims=True)).astype(BF16)
        o = jnp.dot(p, vs[h], preferred_element_type=F32)
        prompt.append(jnp.where(live, o, 0.0))
    pos = lax.broadcasted_iota(jnp.int32, (8, span), 1)
    for d in range(2):
        n = 96 + d
        kv = cache[d]
        self_s = []
        for h in range(3):
            q_bd[h:h + 1, h * 128:(h + 1) * 128] = qs[h][n:n + 1].astype(F32)
            self_s.append(
                jnp.sum(qs[h][n:n + 1].astype(F32) * ks[h][n:n + 1].astype(F32), axis=1, keepdims=True)
            )
        own = jnp.concatenate(self_s + [jnp.zeros((5, 1), F32)], axis=0) * scale
        s = lax.dot_general(
            q_bd[...].astype(BF16), kv, (((1,), (1,)), ((), ())), preferred_element_type=F32
        ) * scale
        ok = (pos % 2 == 0) & (pos < 2 * cache_lengths[d])
        s = jnp.where(ok, s, -1e30)
        top = jnp.maximum(jnp.max(s, axis=1, keepdims=True), own)
        e = jnp.where(ok, jnp.exp(s - top), 0.0)
        mine = jnp.exp(own - top)
        total = jnp.sum(e, axis=1, keepdims=True) + mine
        p = pltpu.roll(e / total, 1, 1).astype(BF16)
        mine = (mine / total).astype(BF16).astype(F32)
        o = jnp.dot(p, kv, preferred_element_type=F32)
        for h in range(3):
            got = o[h:h + 1, h * 128:(h + 1) * 128] + mine[h:h + 1] * vs[h][n:n + 1].astype(F32)
            prompt[h] = jnp.where(row == n, got, prompt[h])
    for h in range(3):
        out[:, h * 128:(h + 1) * 128] = prompt[h].astype(BF16)


def attend(table, lengths, cache_lengths, sums, lows, up_all, bias, cache):
    return pl.pallas_call(
        attend_kernel,
        out_shape=jax.ShapeDtypeStruct((PAD, 384), BF16),
        in_specs=[SMEM_SPEC] * 3 + [VMEM_SPEC] * 5,
        out_specs=VMEM_SPEC,
        scratch_shapes=[pltpu.VMEM((8, 384), F32)],
        compiler_params=pltpu.CompilerParams(vmem_limit_bytes=LIMIT),
        name="attend",
    )(table, lengths, cache_lengths, sums, lows, up_all, bias, cache)


def collect_kernel(att, every, loc, send, recv):
    z, c, m = place()
    barrier = pltpu.get_barrier_semaphore()
    signal(barrier, at((z + 1) % NZ, c, m))
    signal(barrier, at((z + NZ - 1) % NZ, c, m))
    own = pltpu.make_async_copy(att, every.at[z], loc)
    own.start()
    own.wait()
    pl.semaphore_wait(barrier, 2)
    hop = ring_gather(z, c, m, every, send, recv)
    for way in range(2):
        hop(way, 0).start()
    for way, s in ring_steps():
        hop(way, s).wait()
        if s + 1 < (4, 3)[way]:
            hop(way, s + 1).start()


def collect(att):
    dma = pltpu.SemaphoreType.DMA
    return pl.pallas_call(
        collect_kernel,
        out_shape=jax.ShapeDtypeStruct((NZ, *att.shape), BF16),
        in_specs=[VMEM_SPEC],
        out_specs=VMEM_SPEC,
        scratch_shapes=[dma, dma((2, 4)), dma((2, 4))],
        compiler_params=pltpu.CompilerParams(collective_id=2, has_side_effects=True, vmem_limit_bytes=LIMIT),
        name="collect",
    )(att)


def mix_kernel(every, wo_both, out):
    a = every[...].reshape(NZ * PAD, every.shape[2])
    for f in range(2):
        o = lax.dot_general(a, wo_both[f], (((1,), (1,)), ((), ())), preferred_element_type=F32)
        o = o.astype(BF16).reshape(NZ, PAD, o.shape[1])
        for d in range(NZ):
            out[2 * d + f] = o[d]


def mix(every, wo_both):
    return pl.pallas_call(
        mix_kernel,
        out_shape=jax.ShapeDtypeStruct((NM, PAD, wo_both.shape[1]), BF16),
        in_specs=[VMEM_SPEC] * 2,
        out_specs=VMEM_SPEC,
        compiler_params=pltpu.CompilerParams(vmem_limit_bytes=LIMIT),
        name="mix",
    )(every, wo_both)


def scatter_kernel(pieces, tok, bias, out, came, total, back, loc, send, recv, pm_send, pm_recv):
    z, c, m = place()
    tz, tm = m // 2, 2 * z + m % 2
    target = at(tz, c, tm)
    away = tz != z
    rows = tok.shape[0]
    barrier = pltpu.get_barrier_semaphore()
    plane_signal(barrier, z, c, m)

    @pl.when(away)
    def _():
        signal(barrier, target)

    pl.semaphore_wait(barrier, NM - 1 + jnp.minimum(jnp.abs(tz - z), 1))

    def give(k):
        to = (m + k) % NM
        return remote(pieces.at[to], came.at[k], send.at[k], recv.at[k], at(z, c, to))

    def start(k, carry):
        give(k).start()
        return carry

    lax.fori_loop(1, NM, start, 0)
    total[...] = pieces[m].astype(F32)

    def add(k, carry):
        give(k).wait()
        total[...] += came[k].astype(F32)
        return carry

    lax.fori_loop(1, NM, add, 0)
    perm = remote(total, back, pm_send, pm_recv, target)
    keep = pltpu.make_async_copy(total, back, loc)

    @pl.when(away)
    def _():
        perm.start()
        perm.wait()

    @pl.when(jnp.logical_not(away))
    def _():
        keep.start()
        keep.wait()

    out[...] = (tok[...].astype(F32) + back[0:rows, :] + bias[...]).astype(BF16)


def scatter(pieces, tok, bias):
    dma = pltpu.SemaphoreType.DMA
    return pl.pallas_call(
        scatter_kernel,
        out_shape=jax.ShapeDtypeStruct(tok.shape, BF16),
        in_specs=[VMEM_SPEC] * 3,
        out_specs=VMEM_SPEC,
        scratch_shapes=[
            pltpu.VMEM(pieces.shape, BF16),
            pltpu.VMEM(pieces.shape[1:], F32),
            pltpu.VMEM(pieces.shape[1:], F32),
            dma, dma((NM,)), dma((NM,)), dma, dma,
        ],
        compiler_params=pltpu.CompilerParams(collective_id=3, has_side_effects=True, vmem_limit_bytes=LIMIT),
        name="scatter",
    )(pieces, tok, bias)


def on_device(
    tokens,
    layernorm_scale,
    layernorm_bias,
    query_key_value_weight,
    query_key_value_bias,
    adapter_down_weight,
    adapter_up_weight,
    adapter_index_table,
    prompt_length_list,
    cache,
    cache_length_list,
    output_weight,
    output_bias,
):
    cols = tokens.shape[1]
    m = lax.axis_index("mp")
    gains = jnp.stack(
        [lax.dynamic_slice_in_dim(v, m * cols, cols, 0) for v in (layernorm_scale, layernorm_bias)]
    )
    gathered, normed, w_both, wo_both, down_all, up_all = spread(
        tokens, gains, query_key_value_weight, output_weight.T,
        adapter_down_weight.transpose(0, 2, 1), adapter_up_weight,
    )
    part, low = project(adapter_index_table, gathered, normed, w_both, down_all)
    sums, lows = reduce(part, low)
    bias = query_key_value_bias.reshape(9, 1, 128)
    att = attend(
        adapter_index_table, prompt_length_list, cache_length_list, sums, lows, up_all, bias,
        cache.reshape(2, cache.shape[1] * 2, cache.shape[3]),
    )
    every = collect(att)
    pieces = mix(every, wo_both)
    return scatter(pieces, tokens, output_bias[None])


def solution(mesh):
    placed = (
        P("req", "mp"),
        P(),
        P(),
        P(None, "req", "mp"),
        P(None, "mp"),
        P("req", "mp", None),
        P("req", None, None, "mp"),
        P("req", None),
        P("req"),
        P("req", None, None, "mp"),
        P("req"),
        P("mp", "req"),
        P("mp"),
    )
    return jax.shard_map(
        on_device, mesh=mesh, in_specs=placed, out_specs=P("req", "mp"), check_vma=False
    )
```
